256 devices in a mesh: row: 16 (over x, z_lo, core), col: 16 (over z_hi, y).
Axes of the slice: x: 4, y: 4, z: 8 (z_hi: 4, z_lo: 2; z = z_hi * 2 + z_lo), core: 2. Of those that a mesh axis runs over, the one named last changes fastest.
Arguments:
- iterate: bfloat16 [4096, 8192], P('row', 'col'), may hold values from -0.5 to 0.5, as said below
Outputs:
- update: float32 [4096, 8192], P('row', 'col')
The draws below stay inside these ranges and needn't reach their ends.
Inputs may be any that keep to these rules, and one draw needn't show every extreme that they name: One iterate of the orthogonalization.
All inputs are finite; a program needn't handle non-finite values.
Results may differ from the reference program's by a relative error of at most 0.0041.
Values may be sent and summed in bfloat16 or wider, within the bound.
No kernel may reach another device: no remote copies, remote signals or barrier semaphores. Data moves between devices by JAX's collectives and lax.ppermute only.
A program may use at most 64 MiB of HBM per device.

```python
import math
import jax
import jax.numpy as jnp

ROWS = 4096
COLS = 8192


def draw_iterate(key, part):
    first = jax.random.fold_in(key, 0)
    values = jax.random.normal(first, (ROWS, COLS), jnp.float32)
    values = jnp.clip(values, -6.0, 6.0) * (0.7 / jnp.sqrt(jnp.float32(COLS)))
    return values.astype(jnp.bfloat16)


def setup_inputs(seed: int = 0) -> dict:
    seeds = jax.random.split(jax.random.key(seed), 2)
    iterate = draw_iterate(jax.random.fold_in(seeds[1], 71), 0)
    return {"iterate": iterate}


coef_a = 3.4445
coef_b = -4.775
coef_c = 2.0315

def reference(iterate):
    gram = jnp.dot(iterate, iterate.T, preferred_element_type=jnp.float32).astype(jnp.bfloat16)
    square = jnp.dot(gram, gram, preferred_element_type=jnp.float32)
    poly = (coef_b * gram.astype(jnp.float32) + coef_c * square).astype(jnp.bfloat16)
    mixed = jnp.dot(poly, iterate, preferred_element_type=jnp.float32)
    return math.sqrt(COLS) * (coef_a * iterate.astype(jnp.float32) + mixed)
```

```python
import math

import jax
import jax.numpy as jnp
from jax import lax
from jax.sharding import Mesh
from jax.sharding import PartitionSpec as P

COLS = 8192

coef_a = 3.4445
coef_b = -4.775
coef_c = 2.0315

CHIPS = ("x", "zl")
ROW = ("x", "zl", "core")
COL = ("zh", "y")


def gather(block, axes, n):
    copies = jnp.broadcast_to(block[None], (n, *block.shape))
    got = lax.all_to_all(copies, axes, 0, 0)
    return got.reshape(n * block.shape[0], *block.shape[1:])


def scatter_sum(part, axes, n):
    pieces = part.reshape(n, part.shape[0] // n, *part.shape[1:])
    got = lax.all_to_all(pieces, axes, 0, 0)
    return jnp.sum(got.astype(jnp.float32), axis=0).astype(jnp.bfloat16)


def matmul(a, b, dims):
    return lax.dot_general(a, b, (dims, ((), ())), preferred_element_type=jnp.float32)


def core_sum(part, core):
    half = part.shape[0] // 2
    mine = lax.dynamic_slice_in_dim(part, core * half, half, 0)
    other = lax.dynamic_slice_in_dim(part, (1 - core) * half, half, 0)
    return mine + lax.ppermute(other, "core", [(0, 1), (1, 0)])


def per_device(iterate):
    core = lax.axis_index("core")
    own = lax.all_gather(iterate, "core", axis=0, tiled=True)
    panel = gather(iterate, CHIPS, 8)
    gram = matmul(panel, own, ((1,), (1,))).astype(jnp.bfloat16)
    gram = scatter_sum(gram, "y", 4)
    gram = scatter_sum(gram, "zh", 4)
    gram = gather(gram, "zh", 4)
    gram = gather(gram, "y", 4)
    inner = core_sum(matmul(gram, panel, ((0,), (0,))), core)
    mine = iterate.astype(jnp.float32)
    inner = (coef_b * mine + coef_c * inner).astype(jnp.bfloat16)
    panel = gather(inner, CHIPS, 8)
    mixed = core_sum(matmul(gram, panel, ((0,), (0,))), core)
    return math.sqrt(COLS) * (coef_a * mine + mixed)


def solution(mesh):
    fine = Mesh(mesh.devices.reshape(4, 2, 2, 4, 4), (*ROW, *COL))
    placed = P(ROW, COL)
    return jax.shard_map(
        per_device, mesh=fine, in_specs=(placed,), out_specs=placed, check_vma=False
    )
```

```python
import functools
import math

import jax
import jax.numpy as jnp
from jax import lax
from jax.experimental import pallas as pl
from jax.experimental.pallas import tpu as pltpu
from jax.sharding import Mesh
from jax.sharding import PartitionSpec as P

COLS = 8192

coef_a = 3.4445
coef_b = -4.775
coef_c = 2.0315

ROW = ("x", "zl", "core")
COL = ("zh", "y")
BF, F32 = jnp.bfloat16, jnp.float32
ANY = pl.BlockSpec(memory_space=pl.ANY)
VMEM = pl.BlockSpec(memory_space=pltpu.VMEM)


def fetch(axis, k):
    return [((i + k) % 4, i) for i in range(4)]


def swap(array, axis):
    return lax.ppermute(array, axis, [(0, 1), (1, 0)])


def around(array, axis):
    return [array] + [lax.ppermute(array, axis, fetch(axis, k)) for k in (1, 3, 2)]


def panel_copies(blocks, panel, sems):
    y = lax.axis_index("y")
    copies = []
    for n, j in enumerate((0, 1, 3, 2)):
        slot = lax.rem(j - y + 4, 4)
        copies.append(pltpu.make_async_copy(blocks[n], panel.at[slot], sems.at[n]))
    return copies


def gram_kernel(mine, other, b0, b1, b3, b2, o0, o1, o2, o3, own, panel, sems):
    core, zh = lax.axis_index("core"), lax.axis_index("zh")
    copies = panel_copies((b0, b1, b3, b2), panel, sems)
    for n, (ref, half) in enumerate(((mine, core), (other, 1 - core))):
        for i in range(2):
            place = lax.rem(half * 2 + i - zh + 4, 4)
            rows = pl.ds(pl.multiple_of(place * 128, 128), 128)
            copies.append(
                pltpu.make_async_copy(ref.at[pl.ds(i * 128, 128)], own.at[rows], sems.at[4 + 2 * n + i])
            )
    for copy in copies:
        copy.start()
    for copy in copies:
        copy.wait()
    for p, out in enumerate((o0, o1, o2, o3)):
        out[...] = lax.dot_general(
            own[...], panel[p], (((1,), (1,)), ((), ())), preferred_element_type=F32
        ).astype(BF)


def gram_pieces(mine, other, blocks):
    return pl.pallas_call(
        gram_kernel,
        out_shape=[jax.ShapeDtypeStruct((512, 256), BF)] * 4,
        in_specs=[ANY] * 6,
        out_specs=[VMEM] * 4,
        scratch_shapes=[
            pltpu.VMEM((512, 512), BF),
            pltpu.VMEM((4, 256, 512), BF),
            pltpu.SemaphoreType.DMA((8,)),
        ],
        cost_estimate=pl.CostEstimate(flops=2**29, bytes_accessed=5 * 2**19, transcendentals=0),
        name="gram",
    )(mine, other, *blocks)


def sum_kernel(a, b, c, d, o0, o1, o2, o3):
    for k, out in enumerate((o0, o1, o2, o3)):
        rows = pl.ds(k * 128, 128)
        total = (a[rows].astype(F32) + b[rows].astype(F32)) + (c[rows].astype(F32) + d[rows].astype(F32))
        out[...] = total.astype(BF)


def sum_pieces(pieces):
    return pl.pallas_call(
        sum_kernel,
        out_shape=[jax.ShapeDtypeStruct((128, 256), BF)] * 4,
        in_specs=[VMEM] * 4,
        out_specs=[VMEM] * 4,
        cost_estimate=pl.CostEstimate(flops=2**19, bytes_accessed=5 * 2**18, transcendentals=0),
        name="sum_y",
    )(*pieces)


def apply_kernel(*refs):
    gram, blocks = refs[:8], refs[8:16]
    mine, other, panel, total, sems = refs[16:]
    core, zh, y = lax.axis_index("core"), lax.axis_index("zh"), lax.axis_index("y")
    copies = panel_copies(blocks[:4], panel.at[0], sems.at[0])
    copies += panel_copies(blocks[4:], panel.at[1], sems.at[1])
    for copy in copies:
        copy.start()
    for copy in copies:
        copy.wait()
    for k in range(4):
        rows = pl.ds(k * 128, 128)
        acc = jnp.zeros((128, 512), F32)
        for s in range(2):
            for n, p in enumerate((0, 1, 3, 2)):
                acc += jnp.dot(gram[4 * s + n][rows], panel[s, p], preferred_element_type=F32)
        place = lax.rem(zh + k, 4)
        total[pl.ds(pl.multiple_of(place * 128, 128), 128)] = acc
    mine[...] = total[pl.ds(pl.multiple_of(core * 256, 256), 256)]
    other[...] = total[pl.ds(pl.multiple_of((1 - core) * 256, 256), 256)]


def apply(gram, blocks):
    mine, other = pl.pallas_call(
        apply_kernel,
        out_shape=[jax.ShapeDtypeStruct((256, 512), F32)] * 2,
        in_specs=[VMEM] * 8 + [ANY] * 8,
        out_specs=[VMEM] * 2,
        scratch_shapes=[
            pltpu.VMEM((2, 4, 256, 512), BF),
            pltpu.VMEM((512, 512), F32),
            pltpu.SemaphoreType.DMA((2, 4)),
        ],
        cost_estimate=pl.CostEstimate(flops=2**30, bytes_accessed=5 * 2**20, transcendentals=0),
        name="apply",
    )(*gram, *blocks)
    return mine + swap(other, "core")


def gather(block):
    partner = swap(block, "zl")
    return around(block, "x"), around(partner, "x")


def to_y(pieces):
    moved = [lax.ppermute(pieces[p], "y", [(i, (i + p) % 4) for i in range(4)]) for p in (1, 3, 2)]
    return [pieces[0], *moved]


def to_zh(pieces):
    moved = [lax.ppermute(pieces[p], "zh", [(i, (i + p) % 4) for i in range(4)]) for p in (1, 3, 2)]
    return sum(piece.astype(F32) for piece in [pieces[0], *moved]).astype(BF)


def from_zh(block):
    got = around(block, "zh")
    return jnp.concatenate([got[0], got[1], got[3], got[2]], axis=0)


def per_device(iterate):
    other = swap(iterate, "core")
    streams = gather(iterate)
    gram = []
    for blocks in streams:
        pieces = to_y(gram_pieces(iterate, other, blocks))
        block = from_zh(to_zh(sum_pieces(pieces)))
        gram += around(block, "y")
    inner = apply(gram, [*streams[0], *streams[1]])
    streams = gather(inner.astype(BF))
    mixed = apply(gram, [*streams[0], *streams[1]])
    mine = iterate.astype(F32)
    return math.sqrt(COLS) * (coef_a * mine + (coef_b * inner + coef_c * mixed))


def solution(mesh):
    fine = Mesh(mesh.devices.reshape(4, 2, 2, 4, 4), (*ROW, *COL))
    placed = P(ROW, COL)
    return jax.shard_map(
        per_device, mesh=fine, in_specs=(placed,), out_specs=placed, check_vma=False
    )
```

```python
import math

import jax
import jax.numpy as jnp
from jax import lax
from jax.sharding import Mesh
from jax.sharding import PartitionSpec as P

COLS = 8192

coef_a = 3.4445
coef_b = -4.775
coef_c = 2.0315

ROW = ("x", "zl", "core")
COL = ("zh", "y")
BF, F32 = jnp.bfloat16, jnp.float32


def swap(array, axis):
    return lax.ppermute(array, axis, [(0, 1), (1, 0)])


def send(array, axis, k):
    return lax.ppermute(array, axis, [(i, (i + k) % 4) for i in range(4)]) if k else array


def around(array, axis):
    got = {k: send(array, axis, (4 - k) % 4) for k in (0, 1, 3, 2)}
    return [got[k] for k in range(4)]


def scatter_sum(pieces, axis):
    got = [send(pieces[k], axis, k).astype(F32) for k in (0, 1, 3, 2)]
    return ((got[0] + got[1]) + (got[2] + got[3])).astype(BF)


def chunks(array):
    return jnp.split(array, 4, axis=0)


def window(parts, first, count):
    rows = parts[0].shape[0]
    ring = jnp.concatenate([*parts, *parts[: count - 1]], axis=0)
    return lax.dynamic_slice_in_dim(ring, first * rows, count * rows, 0)


def matmul(a, b, dims):
    return lax.dot_general(a, b, (dims, ((), ())), preferred_element_type=F32)


def panels_of(block):
    partner = swap(block, "zl")
    return [jnp.concatenate(around(b, "x"), axis=0) for b in (block, partner)]


def apply(gram, panels):
    other = sum(matmul(g[1], panel, ((1,), (0,))) for g, panel in zip(gram, panels))
    mine = sum(matmul(g[0], panel, ((1,), (0,))) for g, panel in zip(gram, panels))
    return mine + swap(other, "core")


def per_device(iterate):
    core, y, zh = (lax.axis_index(a) for a in ("core", "y", "zh"))
    other = swap(iterate, "core")
    panels = panels_of(iterate)
    halves = [*jnp.split(iterate, 2), *jnp.split(other, 2)]
    own = window(halves, lax.rem(y - 2 * core + 4, 4), 4)
    own = [window(chunks(rows), zh, 4) for rows in chunks(own)]
    gram = []
    for panel in panels:
        pieces = [matmul(rows, panel, ((1,), (1,))).astype(BF) for rows in own]
        part = scatter_sum(pieces, "y")
        part = scatter_sum(chunks(part), "zh")
        rows = window(around(part, "zh"), lax.rem(4 - zh, 4), 4)
        ring = around(rows, "y")
        first = lax.rem(2 * core - y + 4, 4)
        gram.append((window(ring, first, 2), window(ring, lax.rem(first + 2, 4), 2)))
    inner = apply(gram, panels)
    mixed = apply(gram, panels_of(inner.astype(BF)))
    mine = iterate.astype(F32)
    return math.sqrt(COLS) * (coef_a * mine + (coef_b * inner + coef_c * mixed))


def solution(mesh):
    fine = Mesh(mesh.devices.reshape(4, 2, 2, 4, 4), (*ROW, *COL))
    placed = P(ROW, COL)
    return jax.shard_map(
        per_device, mesh=fine, in_specs=(placed,), out_specs=placed, check_vma=False
    )
```

```python
import math

import jax
import jax.numpy as jnp
from jax import lax
from jax.sharding import Mesh
from jax.sharding import PartitionSpec as P

COLS = 8192

coef_a = 3.4445
coef_b = -4.775
coef_c = 2.0315

ROW = ("x", "zl", "core")
COL = ("zh", "y")
BF, F32 = jnp.bfloat16, jnp.float32


def swap(array, axis):
    return lax.ppermute(array, axis, [(0, 1), (1, 0)])


def send(array, axis, k):
    return lax.ppermute(array, axis, [(i, (i + k) % 4) for i in range(4)]) if k else array


def around(array, axis):
    got = {k: send(array, axis, (4 - k) % 4) for k in (0, 1, 3, 2)}
    return [got[k] for k in range(4)]


def add(got):
    got = [g.astype(F32) for g in got]
    return ((got[0] + got[1]) + (got[2] + got[3])).astype(BF)


def scatter_sum(pieces, axis):
    return add([send(pieces[k], axis, k) for k in range(4)])


def exchange(pieces, axis):
    return lax.all_to_all(pieces, axis, 0, 0)


def chunks(array):
    return jnp.split(array, 4, axis=0)


def window(parts, first, count):
    rows = parts[0].shape[0]
    ring = jnp.concatenate([*parts, *parts[: count - 1]], axis=0)
    return lax.dynamic_slice_in_dim(ring, first * rows, count * rows, 0)


def matmul(a, b, dims):
    return lax.dot_general(a, b, (dims, ((), ())), preferred_element_type=F32)


def panels_of(block):
    partner = swap(block, "zl")
    return [jnp.concatenate(around(b, "x"), axis=0) for b in (block, partner)]


def apply(core, gram, panels):
    product = sum(matmul(g, panel, ((1,), (0,))) for g, panel in zip(gram, panels))
    mine = lax.dynamic_slice_in_dim(product, core * 256, 256, 0)
    other = lax.dynamic_slice_in_dim(product, (1 - core) * 256, 256, 0)
    return mine + swap(other, "core")


def per_device(iterate):
    core, zh = lax.axis_index("core"), lax.axis_index("zh")
    other = swap(iterate, "core")
    panels = panels_of(iterate)
    own = window([iterate, other, iterate, other], core, 2)
    own = jnp.concatenate([window(chunks(rows), zh, 4) for rows in chunks(own)], axis=0)
    gram = []
    for panel in panels:
        pieces = matmul(own, panel, ((1,), (1,))).astype(BF)
        part = add(exchange(pieces.reshape(4, 128, 1024), "y"))
        part = scatter_sum(chunks(part), "zh")
        rows = window(around(part, "zh"), lax.rem(4 - zh, 4), 4)
        copies = jnp.broadcast_to(rows[None], (4, 128, 1024))
        gram.append(exchange(copies, "y").reshape(512, 1024))
    inner = apply(core, gram, panels)
    mixed = apply(core, gram, panels_of(inner.astype(BF)))
    mine = iterate.astype(F32)
    return math.sqrt(COLS) * (coef_a * mine + (coef_b * inner + coef_c * mixed))


def solution(mesh):
    fine = Mesh(mesh.devices.reshape(4, 2, 2, 4, 4), (*ROW, *COL))
    placed = P(ROW, COL)
    return jax.shard_map(
        per_device, mesh=fine, in_specs=(placed,), out_specs=placed, check_vma=False
    )
```

```python
import math

import jax
import jax.numpy as jnp
from jax import lax
from jax.sharding import Mesh
from jax.sharding import PartitionSpec as P

COLS = 8192

coef_a = 3.4445
coef_b = -4.775
coef_c = 2.0315

ROW = ("x", "zl", "core")
COL = ("zh", "y")
BF, F32 = jnp.bfloat16, jnp.float32


def swap(array, axis):
    return lax.ppermute(array, axis, [(0, 1), (1, 0)])


def send(array, axis, k):
    return lax.ppermute(array, axis, [(i, (i + k) % 4) for i in range(4)]) if k else array


def around(array, axis):
    got = {k: send(array, axis, (4 - k) % 4) for k in (0, 1, 3, 2)}
    return [got[k] for k in range(4)]


def exchange(pieces, axis):
    return lax.all_to_all(pieces, axis, 0, 0)


def chunks(array):
    return jnp.split(array, 4, axis=0)


def window(parts, first, count):
    rows = parts[0].shape[0]
    ring = jnp.concatenate([*parts, *parts[: count - 1]], axis=0)
    return lax.dynamic_slice_in_dim(ring, first * rows, count * rows, 0)


def matmul(a, b, dims):
    return lax.dot_general(a, b, (dims, ((), ())), preferred_element_type=F32)


def panels_of(block):
    partner = swap(block, "zl")
    return [jnp.concatenate(around(b, "x"), axis=0) for b in (block, partner)]


def apply(core, gram, panels):
    product = sum(matmul(g, panel, ((1,), (0,))) for g, panel in zip(gram, panels))
    mine = lax.dynamic_slice_in_dim(product, core * 256, 256, 0)
    other = lax.dynamic_slice_in_dim(product, (1 - core) * 256, 256, 0)
    return mine + swap(other, "core")


def per_device(iterate):
    core, zh = lax.axis_index("core"), lax.axis_index("zh")
    other = swap(iterate, "core")
    panels = panels_of(iterate)
    own = window([iterate, other, iterate, other], core, 2)
    gram = []
    for panel in panels:
        pieces = matmul(own, panel, ((1,), (1,))).astype(BF)
        part = exchange(pieces.reshape(16, 32, 1024), ("y", "zh")).astype(F32)
        part = jnp.sum(part, axis=0).astype(BF)
        rows = window(around(part, "zh"), lax.rem(4 - zh, 4), 4)
        copies = jnp.broadcast_to(rows[None], (4, 128, 1024))
        gram.append(exchange(copies, "y").reshape(512, 1024))
    inner = apply(core, gram, panels)
    mixed = apply(core, gram, panels_of(inner.astype(BF)))
    mine = iterate.astype(F32)
    return math.sqrt(COLS) * (coef_a * mine + (coef_b * inner + coef_c * mixed))


def solution(mesh):
    fine = Mesh(mesh.devices.reshape(4, 2, 2, 4, 4), (*ROW, *COL))
    placed = P(ROW, COL)
    return jax.shard_map(
        per_device, mesh=fine, in_specs=(placed,), out_specs=placed, check_vma=False
    )
```

```python
import math

import jax
import jax.numpy as jnp
from jax import lax
from jax.sharding import Mesh
from jax.sharding import PartitionSpec as P

COLS = 8192

coef_a = 3.4445
coef_b = -4.775
coef_c = 2.0315

ROW = ("x", "zl", "core")
COL = ("zh", "y")
BF, F32 = jnp.bfloat16, jnp.float32


def swap(array, axis):
    return lax.ppermute(array, axis, [(0, 1), (1, 0)])


def send(array, axis, k):
    return lax.ppermute(array, axis, [(i, (i + k) % 4) for i in range(4)]) if k else array


def around(array, axis):
    got = {k: send(array, axis, (4 - k) % 4) for k in (0, 1, 3, 2)}
    return [got[k] for k in range(4)]


def exchange(pieces, axis):
    return lax.all_to_all(pieces, axis, 0, 0)


def chunks(array):
    return jnp.split(array, 4, axis=0)


def window(parts, first, count):
    rows = parts[0].shape[0]
    ring = jnp.concatenate([*parts, *parts[: count - 1]], axis=0)
    return lax.dynamic_slice_in_dim(ring, first * rows, count * rows, 0)


def matmul(a, b, dims):
    return lax.dot_general(a, b, (dims, ((), ())), preferred_element_type=F32)


def panels_of(block):
    partner = swap(block, "zl")
    panel = jnp.concatenate(around(block, "x"), axis=0)
    panel, partner = lax.optimization_barrier((panel, partner))
    return [panel, jnp.concatenate(around(partner, "x"), axis=0)]


def apply(core, gram, panels):
    product = sum(matmul(g, panel, ((1,), (0,))) for g, panel in zip(gram, panels))
    mine = lax.dynamic_slice_in_dim(product, core * 256, 256, 0)
    other = lax.dynamic_slice_in_dim(product, (1 - core) * 256, 256, 0)
    return mine + swap(other, "core")


def per_device(iterate):
    core, zh = lax.axis_index("core"), lax.axis_index("zh")
    other = swap(iterate, "core")
    panels = panels_of(iterate)
    own = window([iterate, other, iterate, other], core, 2)
    own = own.reshape(4, 4, 32, 512).swapaxes(0, 1).reshape(512, 512)
    gram = []
    for panel in panels:
        pieces = matmul(own, panel, ((1,), (1,))).astype(BF)
        part = exchange(pieces.reshape(16, 32, 1024), COL).astype(F32)
        part = jnp.sum(part, axis=0).astype(BF)
        rows = window(around(part, "zh"), lax.rem(4 - zh, 4), 4)
        copies = jnp.broadcast_to(rows[None], (4, 128, 1024))
        gram.append(exchange(copies, "y").reshape(512, 1024))
    inner = apply(core, gram, panels)
    mixed = apply(core, gram, panels_of(inner.astype(BF)))
    mine = iterate.astype(F32)
    return math.sqrt(COLS) * (coef_a * mine + (coef_b * inner + coef_c * mixed))


def solution(mesh):
    fine = Mesh(mesh.devices.reshape(4, 2, 2, 4, 4), (*ROW, *COL))
    placed = P(ROW, COL)
    return jax.shard_map(
        per_device, mesh=fine, in_specs=(placed,), out_specs=placed, check_vma=False
    )
```

```python
import math

import jax
import jax.numpy as jnp
from jax import lax
from jax.sharding import Mesh
from jax.sharding import PartitionSpec as P

COLS = 8192

coef_a = 3.4445
coef_b = -4.775
coef_c = 2.0315

ROW = ("x", "zl", "core")
COL = ("zh", "y")
BF, F32 = jnp.bfloat16, jnp.float32


def swap(array, axis):
    return lax.ppermute(array, axis, [(0, 1), (1, 0)])


def send(array, axis, k):
    return lax.ppermute(array, axis, [(i, (i + k) % 4) for i in range(4)]) if k else array


def fetch(array, axis, k):
    return send(array, axis, (4 - k) % 4)


def scatter_sum(pieces, axis):
    got = [send(pieces[k], axis, k).astype(F32) for k in (0, 1, 3, 2)]
    return ((got[0] + got[1]) + (got[2] + got[3])).astype(BF)


def around(array, axis):
    return [array] + [fetch(array, axis, k) for k in (1, 2, 3)]


def around_ring(array, axis):
    half = array.shape[0] // 2
    after, before = fetch(array, axis, 1), fetch(array, axis, 3)
    far = [fetch(after[:half], axis, 1), fetch(before[half:], axis, 3)]
    return [array, after, jnp.concatenate(far, axis=0), before]


def chunks(array):
    return jnp.split(array, 4, axis=0)


def window(parts, first, count):
    rows = parts[0].shape[0]
    ring = jnp.concatenate([*parts, *parts[: count - 1]], axis=0)
    return lax.dynamic_slice_in_dim(ring, first * rows, count * rows, 0)


def matmul(a, b, dims):
    return lax.dot_general(a, b, (dims, ((), ())), preferred_element_type=F32)


def panel_of(block):
    partner = swap(block, "zl")
    mine = around(block, "x")
    theirs = [partner, fetch(partner, "x", 1), swap(mine[2], "zl"), fetch(partner, "x", 3)]
    return jnp.concatenate([*mine, *theirs], axis=0)


def apply(gram, panel):
    other = swap(matmul(gram[1], panel, ((1,), (0,))), "core")
    return matmul(gram[0], panel, ((1,), (0,))) + other


def per_device(iterate):
    core, y, zh = (lax.axis_index(a) for a in ("core", "y", "zh"))
    other = swap(iterate, "core")
    panel = panel_of(iterate)
    halves = [*jnp.split(iterate, 2), *jnp.split(other, 2)]
    own = window(halves, lax.rem(y - 2 * core + 4, 4), 4)
    own = [window(chunks(rows), zh, 4) for rows in chunks(own)]
    pieces = [matmul(rows, panel, ((1,), (1,))).astype(BF) for rows in own]
    part = scatter_sum(pieces, "y")
    part = scatter_sum(chunks(part), "zh")
    rows = window(around(part, "zh"), lax.rem(4 - zh, 4), 4)
    ring = around_ring(rows, "y")
    first = lax.rem(2 * core - y + 4, 4)
    gram = window(ring, first, 2), window(ring, lax.rem(first + 2, 4), 2)
    inner = apply(gram, panel)
    mixed = apply(gram, panel_of(inner.astype(BF)))
    mine = iterate.astype(F32)
    return math.sqrt(COLS) * (coef_a * mine + (coef_b * inner + coef_c * mixed))


def solution(mesh):
    fine = Mesh(mesh.devices.reshape(4, 2, 2, 4, 4), (*ROW, *COL))
    placed = P(ROW, COL)
    return jax.shard_map(
        per_device, mesh=fine, in_specs=(placed,), out_specs=placed, check_vma=False
    )
```

```python
import math

import jax
import jax.numpy as jnp
from jax import lax
from jax.sharding import Mesh
from jax.sharding import PartitionSpec as P

COLS = 8192

coef_a = 3.4445
coef_b = -4.775
coef_c = 2.0315

ROW = ("x", "zl", "core")
COL = ("zh", "y")
BF, F32 = jnp.bfloat16, jnp.float32


def swap(array, axis):
    return lax.ppermute(array, axis, [(0, 1), (1, 0)])


def send(array, axis, k):
    return lax.ppermute(array, axis, [(i, (i + k) % 4) for i in range(4)]) if k else array


def fetch(array, axis, k):
    return send(array, axis, (4 - k) % 4)


def scatter_sum(pieces, axis):
    got = [send(pieces[k], axis, k).astype(F32) for k in (0, 1, 3, 2)]
    return ((got[0] + got[1]) + (got[2] + got[3])).astype(BF)


def around(array, axis):
    return [array] + [fetch(array, axis, k) for k in (1, 2, 3)]


def chunks(array):
    return jnp.split(array, 4, axis=0)


def window(parts, first, count):
    rows = parts[0].shape[0]
    ring = jnp.concatenate([*parts, *parts[: count - 1]], axis=0)
    return lax.dynamic_slice_in_dim(ring, first * rows, count * rows, 0)


def matmul(a, b, dims):
    return lax.dot_general(a, b, (dims, ((), ())), preferred_element_type=F32)


def spread(block):
    partner = swap(block, "zl")
    return partner, around(block, "x")


def spread_more(partner, mine):
    return [partner, fetch(partner, "x", 1), swap(mine[2], "zl"), fetch(partner, "x", 3)]


def panel_of(blocks):
    count = blocks[0].shape[0] // 64
    panel = jnp.concatenate([b.reshape(count, 1, 64, 512) for b in blocks], axis=1)
    return panel.reshape(count * 512, 512)


def core_sum(products):
    mine = jnp.concatenate([m for m, _ in products], axis=0)
    other = jnp.concatenate([o for _, o in products], axis=0)
    return mine + swap(other, "core")


def per_device(iterate):
    y, zh = lax.axis_index("y"), lax.axis_index("zh")
    back = lax.rem(4 - y, 4)
    other = swap(iterate, "core")
    partner, blocks = spread(iterate)
    panel = panel_of([*blocks, *spread_more(partner, blocks)])

    own = zip(chunks(window(chunks(iterate), y, 4)), chunks(window(chunks(other), y, 4)))
    own = [window(chunks(jnp.concatenate(rows, axis=0)), zh, 4) for rows in own]
    pieces = [matmul(rows, panel, ((1,), (1,))).astype(BF) for rows in own]
    part = scatter_sum(pieces, "y")
    part = scatter_sum(chunks(part), "zh")
    near = window(around(part, "zh"), lax.rem(4 - zh, 4), 4)
    after, before = fetch(near, "y", 1), fetch(near, "y", 3)
    far = fetch(after[:64], "y", 1), fetch(before[64:], "y", 3)

    def product(rows):
        return matmul(rows, panel, ((1,), (0,)))

    first = core_sum([(m[:64], m[64:]) for m in map(product, (near, after, before))])
    partner, blocks = spread(first.astype(BF))
    partner, *blocks, far_0, far_1 = lax.optimization_barrier((partner, *blocks, *far))
    far = far_0, far_1
    second = core_sum([(product(far[0]), product(far[1]))])
    sent = second.astype(BF)
    panel_1 = panel_of([*blocks, *spread_more(partner, blocks)])
    partner, blocks = spread(sent)
    panel_2 = panel_of([*blocks, *spread_more(partner, blocks)])

    gram = [(near[:64], near[64:]), (after[:64], after[64:]), far, (before[:64], before[64:])]
    inner = window([first[:64], first[64:128], second, first[128:]], back, 4)
    mixed = []
    for rows in zip(*gram):
        rows = window(rows, back, 4)
        c = [lax.dynamic_slice_in_dim(rows, lax.rem(y + p, 4) * 512, 512, 1) for p in range(4)]
        near_3 = jnp.concatenate([c[0], c[1], c[3]], axis=1)
        mixed.append(matmul(near_3, panel_1, ((1,), (0,))) + matmul(c[2], panel_2, ((1,), (0,))))
    mixed = mixed[0] + swap(mixed[1], "core")
    mine = iterate.astype(F32)
    return math.sqrt(COLS) * (coef_a * mine + (coef_b * inner + coef_c * mixed))


def solution(mesh):
    fine = Mesh(mesh.devices.reshape(4, 2, 2, 4, 4), (*ROW, *COL))
    placed = P(ROW, COL)
    return jax.shard_map(
        per_device, mesh=fine, in_specs=(placed,), out_specs=placed, check_vma=False
    )
```

```python
import math

import jax
import jax.numpy as jnp
from jax import lax
from jax.sharding import Mesh
from jax.sharding import PartitionSpec as P

COLS = 8192

coef_a = 3.4445
coef_b = -4.775
coef_c = 2.0315

ROW = ("x", "zl", "core")
COL = ("zh", "y")
BF, F32 = jnp.bfloat16, jnp.float32


def swap(array, axis):
    return lax.ppermute(array, axis, [(0, 1), (1, 0)])


def send(array, axis, k):
    return lax.ppermute(array, axis, [(i, (i + k) % 4) for i in range(4)]) if k else array


def fetch(array, axis, k):
    return send(array, axis, (4 - k) % 4)


def add(got):
    got = [g.astype(F32) for g in got]
    return ((got[0] + got[1]) + (got[2] + got[3])).astype(BF)


def scatter(pieces, axis):
    return [send(pieces[k], axis, k) for k in (0, 1, 3, 2)]


def around(array, axis):
    return [array] + [fetch(array, axis, k) for k in (1, 2, 3)]


def chunks(array):
    return jnp.split(array, 4, axis=0)


def window(parts, first, count):
    rows = parts[0].shape[0]
    ring = jnp.concatenate([*parts, *parts[: count - 1]], axis=0)
    return lax.dynamic_slice_in_dim(ring, first * rows, count * rows, 0)


def matmul(a, b, dims):
    return lax.dot_general(a, b, (dims, ((), ())), preferred_element_type=F32)


def panels_of(block):
    partner = swap(block, "zl")
    mine = around(block, "x")
    theirs = [partner, fetch(partner, "x", 1), swap(mine[2], "zl"), fetch(partner, "x", 3)]
    panels = [jnp.concatenate([b.reshape(4, 1, 64, 512) for b in four], axis=1) for four in (mine, theirs)]
    return [panel.reshape(1024, 512) for panel in panels]


def core_sum(products):
    mine = jnp.concatenate([m for m, _ in products], axis=0)
    other = jnp.concatenate([o for _, o in products], axis=0)
    return mine + swap(other, "core")


def per_device(iterate):
    y, zh = lax.axis_index("y"), lax.axis_index("zh")
    other = swap(iterate, "core")
    panels = panels_of(iterate)

    own = [jnp.concatenate(rows, axis=0) for rows in zip(chunks(iterate), chunks(other))]
    own = [window(chunks(rows), zh, 4) for rows in own]
    pieces = matmul(jnp.concatenate(own, axis=0), panels[0], ((1,), (1,))).astype(BF)
    first = add(lax.all_to_all(pieces.reshape(4, 128, 1024), "y", 0, 0))
    own = chunks(window(own, y, 4))
    pieces = [matmul(rows, panels[1], ((1,), (1,))).astype(BF) for rows in own]
    second = add(scatter(pieces, "y"))
    part = jnp.concatenate([first, second], axis=1)
    part = add(scatter(chunks(part), "zh"))
    near = lax.all_gather(part, "zh", axis=0, tiled=True)
    after, before = fetch(near, "y", 1), fetch(near, "y", 3)
    far = fetch(after[:64], "y", 1), fetch(before[64:], "y", 3)

    panel = jnp.concatenate(panels, axis=0)

    def product(rows):
        return matmul(rows, panel, ((1,), (0,)))

    first = core_sum([(m[:64], m[64:]) for m in map(product, (near, after, before))])
    second = core_sum([(product(far[0]), product(far[1]))])
    inner = [first[:64], first[64:128], second, first[128:]]
    panels = panels_of(jnp.concatenate(inner, axis=0).astype(BF))

    back = lax.rem(4 - y, 4)
    gram = [(near[:64], near[64:]), (after[:64], after[64:]), far, (before[:64], before[64:])]
    mixed = []
    for rows in zip(*gram):
        rows = window(rows, back, 4)
        halves = jnp.split(rows, 2, axis=1)
        halves = [lax.dynamic_slice_in_dim(jnp.concatenate([h, h[:, :768]], axis=1), y * 256, 1024, 1) for h in halves]
        mixed.append(sum(matmul(h, panel, ((1,), (0,))) for h, panel in zip(halves, panels)))
    mixed = mixed[0] + swap(mixed[1], "core")
    mine = iterate.astype(F32)
    inner = window(inner, back, 4)
    return math.sqrt(COLS) * (coef_a * mine + (coef_b * inner + coef_c * mixed))


def solution(mesh):
    fine = Mesh(mesh.devices.reshape(4, 2, 2, 4, 4), (*ROW, *COL))
    placed = P(ROW, COL)
    return jax.shard_map(
        per_device, mesh=fine, in_specs=(placed,), out_specs=placed, check_vma=False
    )
```

```python
import math

import jax
import jax.numpy as jnp
from jax import lax
from jax.sharding import Mesh
from jax.sharding import PartitionSpec as P

COLS = 8192

coef_a = 3.4445
coef_b = -4.775
coef_c = 2.0315

ROW = ("x", "zl", "core")
COL = ("zh", "y")
BF, F32 = jnp.bfloat16, jnp.float32


def swap(array, axis):
    return lax.ppermute(array, axis, [(0, 1), (1, 0)])


def send(array, axis, k):
    return lax.ppermute(array, axis, [(i, (i + k) % 4) for i in range(4)]) if k else array


def fetch(array, axis, k):
    return send(array, axis, (4 - k) % 4)


def add(got):
    got = [g.astype(F32) for g in got]
    return ((got[0] + got[1]) + (got[2] + got[3])).astype(BF)


def scatter(pieces, axis):
    return [send(pieces[k], axis, k) for k in (0, 1, 3, 2)]


def around(array, axis):
    return [array] + [fetch(array, axis, k) for k in (1, 2, 3)]


def chunks(array):
    return jnp.split(array, 4, axis=0)


def window(parts, first, count):
    rows = parts[0].shape[0]
    ring = jnp.concatenate([*parts, *parts[: count - 1]], axis=0)
    return lax.dynamic_slice_in_dim(ring, first * rows, count * rows, 0)


def matmul(a, b, dims):
    return lax.dot_general(a, b, (dims, ((), ())), preferred_element_type=F32)


def panels_of(block):
    partner = swap(block, "zl")
    mine = around(block, "x")
    theirs = [partner, fetch(partner, "x", 1), swap(mine[2], "zl"), fetch(partner, "x", 3)]
    blocks = lax.optimization_barrier([*mine, *theirs])
    panels = [jnp.concatenate([b.reshape(4, 1, 64, 512) for b in four], axis=1) for four in (blocks[:4], blocks[4:])]
    return [panel.reshape(1024, 512) for panel in panels]


def core_sum(products):
    mine = jnp.concatenate([m for m, _ in products], axis=0)
    other = jnp.concatenate([o for _, o in products], axis=0)
    return mine + swap(other, "core")


def per_device(iterate):
    y, zh = lax.axis_index("y"), lax.axis_index("zh")
    other = swap(iterate, "core")
    panels = panels_of(iterate)

    panel = jnp.concatenate(panels, axis=0)

    own = zip(chunks(window(chunks(iterate), y, 4)), chunks(window(chunks(other), y, 4)))
    own = [window(chunks(jnp.concatenate(rows, axis=0)), zh, 4) for rows in own]
    pieces = [matmul(rows, panel, ((1,), (1,))).astype(BF) for rows in own]
    part = add(scatter(pieces, "y"))
    part = add(scatter(chunks(part), "zh"))
    near = lax.all_gather(part, "zh", axis=0, tiled=True)
    after, before = fetch(near, "y", 1), fetch(near, "y", 3)
    sent = lax.optimization_barrier((after[:64], before[64:]))
    far = lax.optimization_barrier((fetch(sent[0], "y", 1), fetch(sent[1], "y", 3)))

    def product(rows):
        return matmul(rows, panel, ((1,), (0,)))

    first = core_sum([(m[:64], m[64:]) for m in map(product, (near, after, before))])
    second = core_sum([(product(far[0]), product(far[1]))])
    inner = [first[:64], first[64:128], second, first[128:]]
    panels = panels_of(jnp.concatenate(inner, axis=0).astype(BF))

    back = lax.rem(4 - y, 4)
    gram = [(near[:64], near[64:]), (after[:64], after[64:]), far, (before[:64], before[64:])]
    mixed = []
    for rows in zip(*gram):
        rows = window(rows, back, 4)
        halves = jnp.split(rows, 2, axis=1)
        halves = [lax.dynamic_slice_in_dim(jnp.concatenate([h, h[:, :768]], axis=1), y * 256, 1024, 1) for h in halves]
        mixed.append(sum(matmul(h, panel, ((1,), (0,))) for h, panel in zip(halves, panels)))
    mixed = mixed[0] + swap(mixed[1], "core")
    mine = iterate.astype(F32)
    inner = window(inner, back, 4)
    return math.sqrt(COLS) * (coef_a * mine + (coef_b * inner + coef_c * mixed))


def solution(mesh):
    fine = Mesh(mesh.devices.reshape(4, 2, 2, 4, 4), (*ROW, *COL))
    placed = P(ROW, COL)
    return jax.shard_map(
        per_device, mesh=fine, in_specs=(placed,), out_specs=placed, check_vma=False
    )
```

```python
import math

import jax
import jax.numpy as jnp
from jax import lax
from jax.sharding import Mesh
from jax.sharding import PartitionSpec as P

COLS = 8192

coef_a = 3.4445
coef_b = -4.775
coef_c = 2.0315

ROW = ("x", "zl", "core")
COL = ("zh", "y")
BF, F32 = jnp.bfloat16, jnp.float32


def swap(array, axis):
    return lax.ppermute(array, axis, [(0, 1), (1, 0)])


def send(array, axis, k):
    return lax.ppermute(array, axis, [(i, (i + k) % 4) for i in range(4)]) if k else array


def fetch(array, axis, k):
    return send(array, axis, (4 - k) % 4)


def add(got):
    got = [g.astype(F32) for g in got]
    return ((got[0] + got[1]) + (got[2] + got[3])).astype(BF)


def scatter(pieces, axis):
    return [send(pieces[k], axis, k) for k in (0, 1, 3, 2)]


def chunks(array):
    return jnp.split(array, 4, axis=0)


def window(parts, first, count):
    rows = parts[0].shape[0]
    ring = jnp.concatenate([*parts, *parts[: count - 1]], axis=0)
    return lax.dynamic_slice_in_dim(ring, first * rows, count * rows, 0)


def matmul(a, b, dims):
    return lax.dot_general(a, b, (dims, ((), ())), preferred_element_type=F32)


def panels_of(block):
    far = fetch(block, "x", 2)
    partner = swap(block, "zl")
    pair = jnp.concatenate([block, partner], axis=0)
    after, before = fetch(pair, "x", 1), fetch(pair, "x", 3)
    blocks = lax.optimization_barrier([pair, after, before, far, swap(far, "zl")])
    mine = [blocks[0][:256], blocks[1][:256], blocks[3], blocks[2][:256]]
    theirs = [blocks[0][256:], blocks[1][256:], blocks[4], blocks[2][256:]]
    panels = [jnp.concatenate([b.reshape(4, 1, 64, 512) for b in four], axis=1) for four in (mine, theirs)]
    return [panel.reshape(1024, 512) for panel in panels]


def core_sum(products):
    mine = jnp.concatenate([m for m, _ in products], axis=0)
    other = jnp.concatenate([o for _, o in products], axis=0)
    return mine + swap(other, "core")


def per_device(iterate):
    y, zh = lax.axis_index("y"), lax.axis_index("zh")
    other = swap(iterate, "core")
    panels = panels_of(iterate)

    panel = jnp.concatenate(panels, axis=0)

    own = zip(chunks(window(chunks(iterate), y, 4)), chunks(window(chunks(other), y, 4)))
    own = [window(chunks(jnp.concatenate(rows, axis=0)), zh, 4) for rows in own]
    pieces = [matmul(rows, panel, ((1,), (1,))).astype(BF) for rows in own]
    part = add(scatter(pieces, "y"))
    part = add(scatter(chunks(part), "zh"))
    near = lax.all_gather(part, "zh", axis=0, tiled=True)
    after, before = fetch(near, "y", 1), fetch(near, "y", 3)
    sent = lax.optimization_barrier((after[:64], before[64:]))
    far = lax.optimization_barrier((fetch(sent[0], "y", 1), fetch(sent[1], "y", 3)))

    def product(rows):
        return matmul(rows, panel, ((1,), (0,)))

    first = core_sum([(m[:64], m[64:]) for m in map(product, (near, after, before))])
    second = core_sum([(product(far[0]), product(far[1]))])
    inner = [first[:64], first[64:128], second, first[128:]]
    panels = panels_of(jnp.concatenate(inner, axis=0).astype(BF))

    back = lax.rem(4 - y, 4)
    gram = [(near[:64], near[64:]), (after[:64], after[64:]), far, (before[:64], before[64:])]
    mixed = []
    for rows in zip(*gram):
        rows = window(rows, back, 4)
        halves = jnp.split(rows, 2, axis=1)
        halves = [lax.dynamic_slice_in_dim(jnp.concatenate([h, h[:, :768]], axis=1), y * 256, 1024, 1) for h in halves]
        mixed.append(sum(matmul(h, panel, ((1,), (0,))) for h, panel in zip(halves, panels)))
    mixed = mixed[0] + swap(mixed[1], "core")
    mine = iterate.astype(F32)
    inner = window(inner, back, 4)
    return math.sqrt(COLS) * (coef_a * mine + (coef_b * inner + coef_c * mixed))


def solution(mesh):
    fine = Mesh(mesh.devices.reshape(4, 2, 2, 4, 4), (*ROW, *COL))
    placed = P(ROW, COL)
    return jax.shard_map(
        per_device, mesh=fine, in_specs=(placed,), out_specs=placed, check_vma=False
    )
```

```python
import math

import jax
import jax.numpy as jnp
from jax import lax
from jax.experimental import pallas as pl
from jax.experimental.pallas import tpu as pltpu
from jax.sharding import Mesh
from jax.sharding import PartitionSpec as P

COLS = 8192

coef_a = 3.4445
coef_b = -4.775
coef_c = 2.0315

ROW = ("x", "zl", "core")
COL = ("zh", "y")
BF, F32 = jnp.bfloat16, jnp.float32


def swap(array, axis):
    return lax.ppermute(array, axis, [(0, 1), (1, 0)])


def send(array, axis, k):
    return lax.ppermute(array, axis, [(i, (i + k) % 4) for i in range(4)]) if k else array


def fetch(array, axis, k):
    return send(array, axis, (4 - k) % 4)


def add(got):
    got = [g.astype(F32) for g in got]
    return ((got[0] + got[1]) + (got[2] + got[3])).astype(BF)


def scatter(pieces, axis):
    return [send(pieces[k], axis, k) for k in (0, 1, 3, 2)]


def chunks(array):
    return jnp.split(array, 4, axis=0)


def window(parts, first, count):
    rows = parts[0].shape[0]
    ring = jnp.concatenate([*parts, *parts[: count - 1]], axis=0)
    return lax.dynamic_slice_in_dim(ring, first * rows, count * rows, 0)


def matmul(a, b, dims):
    return lax.dot_general(a, b, (dims, ((), ())), preferred_element_type=F32)


def blocks_of(block):
    far = fetch(block, "x", 2)
    partner = swap(block, "zl")
    pair = jnp.concatenate([block, partner], axis=0)
    return [pair, far], [fetch(pair, "x", 1), fetch(pair, "x", 3), swap(far, "zl")]


def gram_kernel(own, pair, far, out):
    for q in range(4):
        rows = own[pl.ds(q * 128, 128)]
        out[q, :, :512] = matmul(rows, pair[...], ((1,), (1,))).astype(BF)
        out[q, :, 512:] = matmul(rows, far[...], ((1,), (1,))).astype(BF)


def first_pieces(own, pair, far):
    return pl.pallas_call(
        gram_kernel,
        out_shape=jax.ShapeDtypeStruct((4, 128, 768), BF),
        in_specs=[pl.BlockSpec(memory_space=pltpu.VMEM)] * 3,
        out_specs=pl.BlockSpec(memory_space=pltpu.VMEM),
        cost_estimate=pl.CostEstimate(flops=2**35, bytes_accessed=2**21, transcendentals=0),
        name="gram",
    )(own, pair, far)


def core_sum(products):
    mine = jnp.concatenate([m for m, _ in products], axis=0)
    other = jnp.concatenate([o for _, o in products], axis=0)
    return mine + swap(other, "core")


def per_device(iterate):
    y, zh = lax.axis_index("y"), lax.axis_index("zh")
    back = lax.rem(4 - y, 4)
    other = swap(iterate, "core")
    early, late = blocks_of(iterate)

    own = [jnp.concatenate(rows, axis=0) for rows in zip(chunks(iterate), chunks(other))]
    own = [window(chunks(rows), zh, 4) for rows in own]
    pieces = first_pieces(jnp.concatenate(own, axis=0), *early)
    first = add(lax.all_to_all(pieces, "y", 0, 0))
    panel = jnp.concatenate(late, axis=0)
    pieces = [matmul(rows, panel, ((1,), (1,))).astype(BF) for rows in chunks(window(own, y, 4))]
    second = add(scatter(pieces, "y"))
    part = jnp.concatenate([first, second], axis=1)
    panel = jnp.concatenate([*early, *late], axis=0)
    part = add(scatter(chunks(part), "zh"))
    near = lax.all_gather(part, "zh", axis=0, tiled=True)
    after, before = fetch(near, "y", 1), fetch(near, "y", 3)
    sent = lax.optimization_barrier((after[:64], before[64:]))
    far = lax.optimization_barrier((fetch(sent[0], "y", 1), fetch(sent[1], "y", 3)))

    def product(rows):
        return matmul(rows, panel, ((1,), (0,)))

    first = core_sum([(m[:64], m[64:]) for m in map(product, (near, after, before))])
    second = core_sum([(product(far[0]), product(far[1]))])
    inner = window([first[:64], first[64:128], second, first[128:]], back, 4)

    early, late = blocks_of(inner.astype(BF))
    blocks = lax.optimization_barrier([*early, *late])
    panels = jnp.concatenate(blocks[:2], axis=0), jnp.concatenate(blocks[2:], axis=0)
    gram = [(near[:64], near[64:]), (after[:64], after[64:]), far, (before[:64], before[64:])]
    mixed = []
    for rows in zip(*gram):
        rows = window(rows, back, 4)
        halves = rows[:, :768], rows[:, 768:]
        mixed.append(sum(matmul(h, panel, ((1,), (0,))) for h, panel in zip(halves, panels)))
    mixed = mixed[0] + swap(mixed[1], "core")
    mine = iterate.astype(F32)
    return math.sqrt(COLS) * (coef_a * mine + (coef_b * inner + coef_c * mixed))


def solution(mesh):
    fine = Mesh(mesh.devices.reshape(4, 2, 2, 4, 4), (*ROW, *COL))
    placed = P(ROW, COL)
    return jax.shard_map(
        per_device, mesh=fine, in_specs=(placed,), out_specs=placed, check_vma=False
    )
```

```python
import math

import jax
import jax.numpy as jnp
from jax import lax
from jax.sharding import Mesh
from jax.sharding import PartitionSpec as P

COLS = 8192

coef_a = 3.4445
coef_b = -4.775
coef_c = 2.0315

ROW = ("x", "zl", "core")
COL = ("zh", "y")
BF, F32 = jnp.bfloat16, jnp.float32


def swap(array, axis):
    return lax.ppermute(array, axis, [(0, 1), (1, 0)])


def send(array, axis, k):
    return lax.ppermute(array, axis, [(i, (i + k) % 4) for i in range(4)]) if k else array


def fetch(array, axis, k):
    return send(array, axis, (4 - k) % 4)


def add(got):
    got = [g.astype(F32) for g in got]
    return ((got[0] + got[1]) + (got[2] + got[3])).astype(BF)


def scatter(pieces, axis):
    return [send(pieces[k], axis, k) for k in (0, 1, 3, 2)]


def chunks(array):
    return jnp.split(array, 4, axis=0)


def window(parts, first, count):
    rows = parts[0].shape[0]
    ring = jnp.concatenate([*parts, *parts[: count - 1]], axis=0)
    return lax.dynamic_slice_in_dim(ring, first * rows, count * rows, 0)


def matmul(a, b, dims):
    return lax.dot_general(a, b, (dims, ((), ())), preferred_element_type=F32)


def blocks_of(block):
    far = fetch(block, "x", 2)
    partner = swap(block, "zl")
    pair = jnp.concatenate([block, partner], axis=0)
    return pair, [far, fetch(pair, "x", 1), fetch(pair, "x", 3), swap(far, "zl")]


def core_sum(products):
    mine = jnp.concatenate([m for m, _ in products], axis=0)
    other = jnp.concatenate([o for _, o in products], axis=0)
    return mine + swap(other, "core")


def per_device(iterate):
    y, zh = lax.axis_index("y"), lax.axis_index("zh")
    back = lax.rem(4 - y, 4)
    other = swap(iterate, "core")
    pair, late = blocks_of(iterate)

    own = [jnp.concatenate(rows, axis=0) for rows in zip(chunks(iterate), chunks(other))]
    own = [window(chunks(rows), zh, 4) for rows in own]
    pieces = matmul(jnp.concatenate(own, axis=0), pair, ((1,), (1,))).astype(BF)
    first = add(lax.all_to_all(pieces.reshape(4, 128, 512), "y", 0, 0))
    panel = lax.optimization_barrier(jnp.concatenate(late, axis=0))
    pieces = [matmul(rows, panel, ((1,), (1,))).astype(BF) for rows in chunks(window(own, y, 4))]
    second = add(scatter(pieces, "y"))
    part = jnp.concatenate([first, second], axis=1)
    panel = jnp.concatenate([pair, panel], axis=0)
    part = add(scatter(chunks(part), "zh"))
    near = lax.all_gather(part, "zh", axis=0, tiled=True)
    after, before = fetch(near, "y", 1), fetch(near, "y", 3)
    sent = lax.optimization_barrier((after[:64], before[64:]))
    far = lax.optimization_barrier((fetch(sent[0], "y", 1), fetch(sent[1], "y", 3)))

    def product(rows):
        return matmul(rows, panel, ((1,), (0,)))

    first = core_sum([(m[:64], m[64:]) for m in map(product, (near, after, before))])
    second = core_sum([(product(far[0]), product(far[1]))])
    inner = window([first[:64], first[64:128], second, first[128:]], back, 4)

    pair, late = blocks_of(inner.astype(BF))
    pair, *late = lax.optimization_barrier([pair, *late])
    panels = pair, jnp.concatenate(late, axis=0)
    gram = [(near[:64], near[64:]), (after[:64], after[64:]), far, (before[:64], before[64:])]
    mixed = []
    for rows in zip(*gram):
        rows = window(rows, back, 4)
        halves = rows[:, :512], rows[:, 512:]
        mixed.append(sum(matmul(h, panel, ((1,), (0,))) for h, panel in zip(halves, panels)))
    mixed = mixed[0] + swap(mixed[1], "core")
    mine = iterate.astype(F32)
    return math.sqrt(COLS) * (coef_a * mine + (coef_b * inner + coef_c * mixed))


def solution(mesh):
    fine = Mesh(mesh.devices.reshape(4, 2, 2, 4, 4), (*ROW, *COL))
    placed = P(ROW, COL)
    return jax.shard_map(
        per_device, mesh=fine, in_specs=(placed,), out_specs=placed, check_vma=False
    )
```

```python
import math

import jax
import jax.numpy as jnp
from jax import lax
from jax.sharding import Mesh
from jax.sharding import PartitionSpec as P

COLS = 8192

coef_a = 3.4445
coef_b = -4.775
coef_c = 2.0315

ROW = ("x", "zl", "core")
COL = ("zh", "y")
BF, F32 = jnp.bfloat16, jnp.float32


def swap(array, axis):
    return lax.ppermute(array, axis, [(0, 1), (1, 0)])


def send(array, axis, k):
    return lax.ppermute(array, axis, [(i, (i + k) % 4) for i in range(4)]) if k else array


def fetch(array, axis, k):
    return send(array, axis, (4 - k) % 4)


def add(got):
    got = [g.astype(F32) for g in got]
    return ((got[0] + got[1]) + (got[2] + got[3])).astype(BF)


def scatter(pieces, axis):
    return [send(pieces[k], axis, k) for k in (0, 1, 3, 2)]


def chunks(array):
    return jnp.split(array, 4, axis=0)


def window(parts, first, count):
    rows = parts[0].shape[0]
    ring = jnp.concatenate([*parts, *parts[: count - 1]], axis=0)
    return lax.dynamic_slice_in_dim(ring, first * rows, count * rows, 0)


def matmul(a, b, dims):
    return lax.dot_general(a, b, (dims, ((), ())), preferred_element_type=F32)


def pair_of(block):
    far = fetch(block, "x", 2)
    return jnp.concatenate([block, swap(block, "zl")], axis=0), far


def late_blocks(pair, far):
    return [far, fetch(pair, "x", 1), fetch(pair, "x", 3), swap(far, "zl")]


def core_sum(products):
    mine = jnp.concatenate([m for m, _ in products], axis=0)
    other = jnp.concatenate([o for _, o in products], axis=0)
    return mine + swap(other, "core")


def per_device(iterate):
    y, zh = lax.axis_index("y"), lax.axis_index("zh")
    back = lax.rem(4 - y, 4)
    other = swap(iterate, "core")
    pair, far = pair_of(iterate)

    own = [jnp.concatenate(rows, axis=0) for rows in zip(chunks(iterate), chunks(other))]
    own = [window(chunks(rows), zh, 4) for rows in own]
    pieces = matmul(jnp.concatenate(own, axis=0), pair, ((1,), (1,))).astype(BF)
    pieces, far = lax.optimization_barrier((pieces, far))
    late = late_blocks(pair, far)
    first = add(lax.all_to_all(pieces.reshape(4, 128, 512), "y", 0, 0))
    panel = lax.optimization_barrier(jnp.concatenate(late, axis=0))
    pieces = [matmul(rows, panel, ((1,), (1,))).astype(BF) for rows in chunks(window(own, y, 4))]
    second = add(scatter(pieces, "y"))
    part = jnp.concatenate([first, second], axis=1)
    panel = jnp.concatenate([pair, panel], axis=0)
    part = add(scatter(chunks(part), "zh"))
    near = lax.all_gather(part, "zh", axis=0, tiled=True)
    after, before = fetch(near, "y", 1), fetch(near, "y", 3)
    sent = lax.optimization_barrier((after[:64], before[64:]))
    far = lax.optimization_barrier((fetch(sent[0], "y", 1), fetch(sent[1], "y", 3)))

    def product(rows):
        return matmul(rows, panel, ((1,), (0,)))

    first = core_sum([(m[:64], m[64:]) for m in map(product, (near, after, before))])
    second = core_sum([(product(far[0]), product(far[1]))])
    inner = window([first[:64], first[64:128], second, first[128:]], back, 4)

    pair, last = pair_of(inner.astype(BF))
    pair, *late = lax.optimization_barrier([pair, *late_blocks(pair, last)])
    panels = pair, jnp.concatenate(late, axis=0)
    gram = [(near[:64], near[64:]), (after[:64], after[64:]), far, (before[:64], before[64:])]
    mixed = []
    for rows in zip(*gram):
        rows = window(rows, back, 4)
        halves = rows[:, :512], rows[:, 512:]
        mixed.append(sum(matmul(h, panel, ((1,), (0,))) for h, panel in zip(halves, panels)))
    mixed = mixed[0] + swap(mixed[1], "core")
    mine = iterate.astype(F32)
    return math.sqrt(COLS) * (coef_a * mine + (coef_b * inner + coef_c * mixed))


def solution(mesh):
    fine = Mesh(mesh.devices.reshape(4, 2, 2, 4, 4), (*ROW, *COL))
    placed = P(ROW, COL)
    return jax.shard_map(
        per_device, mesh=fine, in_specs=(placed,), out_specs=placed, check_vma=False
    )
```

```python
import math

import jax
import jax.numpy as jnp
from jax import lax
from jax.sharding import Mesh
from jax.sharding import PartitionSpec as P

COLS = 8192

coef_a = 3.4445
coef_b = -4.775
coef_c = 2.0315

ROW = ("x", "zl", "core")
COL = ("zh", "y")
BF, F32 = jnp.bfloat16, jnp.float32


def swap(array, axis):
    return lax.ppermute(array, axis, [(0, 1), (1, 0)])


def send(array, axis, k):
    return lax.ppermute(array, axis, [(i, (i + k) % 4) for i in range(4)]) if k else array


def fetch(array, axis, k):
    return send(array, axis, (4 - k) % 4)


def add(got):
    got = [g.astype(F32) for g in got]
    return ((got[0] + got[1]) + (got[2] + got[3])).astype(BF)


def scatter(pieces, axis):
    return [send(pieces[k], axis, k) for k in (0, 1, 3, 2)]


def chunks(array):
    return jnp.split(array, 4, axis=0)


def window(parts, first, count):
    rows = parts[0].shape[0]
    ring = jnp.concatenate([*parts, *parts[: count - 1]], axis=0)
    return lax.dynamic_slice_in_dim(ring, first * rows, count * rows, 0)


def matmul(a, b, dims):
    return lax.dot_general(a, b, (dims, ((), ())), preferred_element_type=F32)


def pair_of(block):
    far = fetch(block, "x", 2)
    return jnp.concatenate([block, swap(block, "zl")], axis=0), far


def late_blocks(pair, far):
    return [fetch(pair, "x", 1), fetch(pair, "x", 3), swap(far, "zl")]


def core_sum(products):
    mine = jnp.concatenate([m for m, _ in products], axis=0)
    other = jnp.concatenate([o for _, o in products], axis=0)
    return mine + swap(other, "core")


def per_device(iterate):
    y, zh = lax.axis_index("y"), lax.axis_index("zh")
    back = lax.rem(4 - y, 4)
    other = swap(iterate, "core")
    pair, far = pair_of(iterate)

    own = [jnp.concatenate(rows, axis=0) for rows in zip(chunks(iterate), chunks(other))]
    own = [window(chunks(rows), zh, 4) for rows in own]
    early = lax.optimization_barrier(jnp.concatenate([pair, far], axis=0))
    pieces = matmul(jnp.concatenate(own, axis=0), early, ((1,), (1,))).astype(BF)
    late = late_blocks(pair, far)
    first = add(lax.all_to_all(pieces.reshape(4, 128, 768), "y", 0, 0))
    panel = lax.optimization_barrier(jnp.concatenate(late, axis=0))
    pieces = [matmul(rows, panel, ((1,), (1,))).astype(BF) for rows in chunks(window(own, y, 4))]
    second = add(scatter(pieces, "y"))
    first, second = lax.optimization_barrier((first, second))
    part = jnp.concatenate([first, second], axis=1)
    panel = jnp.concatenate([early, panel], axis=0)
    part = add(scatter(chunks(part), "zh"))
    near = lax.all_gather(part, "zh", axis=0, tiled=True)
    after, before = fetch(near, "y", 1), fetch(near, "y", 3)
    sent = lax.optimization_barrier((after[:64], before[64:]))
    far = lax.optimization_barrier((fetch(sent[0], "y", 1), fetch(sent[1], "y", 3)))

    def product(rows):
        return matmul(rows, panel, ((1,), (0,)))

    first = core_sum([(m[:64], m[64:]) for m in map(product, (near, after, before))])
    second = core_sum([(product(far[0]), product(far[1]))])
    inner = window([first[:64], first[64:128], second, first[128:]], back, 4)

    pair, last = pair_of(inner.astype(BF))
    pair, *late = lax.optimization_barrier([pair, last, *late_blocks(pair, last)])
    panels = jnp.concatenate([pair, late[0]], axis=0), jnp.concatenate(late[1:], axis=0)
    gram = [(near[:64], near[64:]), (after[:64], after[64:]), far, (before[:64], before[64:])]
    mixed = []
    for rows in zip(*gram):
        rows = window(rows, back, 4)
        halves = rows[:, :768], rows[:, 768:]
        mixed.append(sum(matmul(h, panel, ((1,), (0,))) for h, panel in zip(halves, panels)))
    mixed = mixed[0] + swap(mixed[1], "core")
    mine = iterate.astype(F32)
    return math.sqrt(COLS) * (coef_a * mine + (coef_b * inner + coef_c * mixed))


def solution(mesh):
    fine = Mesh(mesh.devices.reshape(4, 2, 2, 4, 4), (*ROW, *COL))
    placed = P(ROW, COL)
    return jax.shard_map(
        per_device, mesh=fine, in_specs=(placed,), out_specs=placed, check_vma=False
    )
```

```python
import math

import jax
import jax.numpy as jnp
from jax import lax
from jax.sharding import Mesh
from jax.sharding import PartitionSpec as P

COLS = 8192

coef_a = 3.4445
coef_b = -4.775
coef_c = 2.0315

ROW = ("x", "zl", "core")
COL = ("zh", "y")
BF, F32 = jnp.bfloat16, jnp.float32


def swap(array, axis):
    return lax.ppermute(array, axis, [(0, 1), (1, 0)])


def send(array, axis, k):
    return lax.ppermute(array, axis, [(i, (i + k) % 4) for i in range(4)]) if k else array


def fetch(array, axis, k):
    return send(array, axis, (4 - k) % 4)


def add(got):
    got = [g.astype(F32) for g in got]
    return ((got[0] + got[1]) + (got[2] + got[3])).astype(BF)


def scatter(pieces, axis):
    return [send(pieces[k], axis, k) for k in (0, 1, 3, 2)]


def chunks(array):
    return jnp.split(array, 4, axis=0)


def window(parts, first, count):
    rows = parts[0].shape[0]
    ring = jnp.concatenate([*parts, *parts[: count - 1]], axis=0)
    return lax.dynamic_slice_in_dim(ring, first * rows, count * rows, 0)


def matmul(a, b, dims):
    return lax.dot_general(a, b, (dims, ((), ())), preferred_element_type=F32)


def pair_of(block):
    far = fetch(block, "x", 2)
    return jnp.concatenate([block, swap(block, "zl")], axis=0), far


def late_blocks(pair, far):
    return [fetch(pair, "x", 1), fetch(pair, "x", 3), swap(far, "zl")]


def core_sum(products):
    mine = jnp.concatenate([m for m, _ in products], axis=0)
    other = jnp.concatenate([o for _, o in products], axis=0)
    return mine + swap(other, "core")


def per_device(iterate):
    y, zh = lax.axis_index("y"), lax.axis_index("zh")
    back = lax.rem(4 - y, 4)
    other = swap(iterate, "core")
    pair, far = pair_of(iterate)

    own = [jnp.concatenate(rows, axis=0) for rows in zip(chunks(iterate), chunks(other))]
    own = [window(chunks(rows), zh, 4) for rows in own]
    own, turned = jnp.concatenate(own, axis=0), window(own, y, 4)
    pair, own, turned = lax.optimization_barrier((pair, own, turned))
    early = lax.optimization_barrier(jnp.concatenate([pair, far], axis=0))
    pieces = matmul(own, early, ((1,), (1,))).astype(BF)
    late = late_blocks(pair, far)
    first = add(lax.all_to_all(pieces.reshape(4, 128, 768), "y", 0, 0))
    panel = lax.optimization_barrier(jnp.concatenate(late, axis=0))
    pieces = [matmul(rows, panel, ((1,), (1,))).astype(BF) for rows in chunks(turned)]
    pieces[0] = lax.optimization_barrier(pieces[0])
    second = add(scatter(pieces, "y"))
    part = jnp.concatenate([first, second], axis=1)
    panel = jnp.concatenate([early, panel], axis=0)
    part = add(scatter(chunks(part), "zh"))
    near = lax.all_gather(part, "zh", axis=0, tiled=True)
    after, before = fetch(near, "y", 1), fetch(near, "y", 3)
    sent = lax.optimization_barrier((after[:64], before[64:]))
    far = lax.optimization_barrier((fetch(sent[0], "y", 1), fetch(sent[1], "y", 3)))

    def product(rows):
        return matmul(rows, panel, ((1,), (0,)))

    first = core_sum([(m[:64], m[64:]) for m in map(product, (near, after, before))])
    second = core_sum([(product(far[0]), product(far[1]))])
    inner = window([first[:64], first[64:128], second, first[128:]], back, 4)

    pair, last = pair_of(inner.astype(BF))
    pair, *late = lax.optimization_barrier([pair, last, *late_blocks(pair, last)])
    panels = jnp.concatenate([pair, late[0]], axis=0), jnp.concatenate(late[1:], axis=0)
    gram = [(near[:64], near[64:]), (after[:64], after[64:]), far, (before[:64], before[64:])]
    mixed = []
    for rows in zip(*gram):
        rows = window(rows, back, 4)
        halves = rows[:, :768], rows[:, 768:]
        mixed.append(sum(matmul(h, panel, ((1,), (0,))) for h, panel in zip(halves, panels)))
    mixed = mixed[0] + swap(mixed[1], "core")
    mine = iterate.astype(F32)
    return math.sqrt(COLS) * (coef_a * mine + (coef_b * inner + coef_c * mixed))


def solution(mesh):
    fine = Mesh(mesh.devices.reshape(4, 2, 2, 4, 4), (*ROW, *COL))
    placed = P(ROW, COL)
    return jax.shard_map(
        per_device, mesh=fine, in_specs=(placed,), out_specs=placed, check_vma=False
    )
```

```python
import math

import jax
import jax.numpy as jnp
from jax import lax
from jax.sharding import Mesh
from jax.sharding import PartitionSpec as P

COLS = 8192

coef_a = 3.4445
coef_b = -4.775
coef_c = 2.0315

ROW = ("x", "zl", "core")
COL = ("zh", "y")
BF, F32 = jnp.bfloat16, jnp.float32


def swap(array, axis):
    return lax.ppermute(array, axis, [(0, 1), (1, 0)])


def send(array, axis, k):
    return lax.ppermute(array, axis, [(i, (i + k) % 4) for i in range(4)]) if k else array


def fetch(array, axis, k):
    return send(array, axis, (4 - k) % 4)


def add(got):
    got = [g.astype(F32) for g in got]
    return ((got[0] + got[1]) + (got[2] + got[3])).astype(BF)


def scatter(pieces, axis):
    return [send(pieces[k], axis, k) for k in (0, 1, 3, 2)]


def chunks(array):
    return jnp.split(array, 4, axis=0)


def window(parts, first, count):
    rows = parts[0].shape[0]
    ring = jnp.concatenate([*parts, *parts[: count - 1]], axis=0)
    return lax.dynamic_slice_in_dim(ring, first * rows, count * rows, 0)


def matmul(a, b, dims):
    return lax.dot_general(a, b, (dims, ((), ())), preferred_element_type=F32)


def pair_of(block):
    far = fetch(block, "x", 2)
    return jnp.concatenate([block, swap(block, "zl")], axis=0), far


def late_blocks(pair, far):
    return [fetch(pair, "x", 1), fetch(pair, "x", 3), swap(far, "zl")]


def core_sum(products):
    mine = jnp.concatenate([m for m, _ in products], axis=0)
    other = jnp.concatenate([o for _, o in products], axis=0)
    return mine + swap(other, "core")


def per_device(iterate):
    y = lax.axis_index("y")
    back = lax.rem(4 - y, 4)
    other = swap(iterate, "core")
    pair, far = pair_of(iterate)

    own = [jnp.concatenate(rows, axis=0) for rows in zip(chunks(iterate), chunks(other))]
    own, turned = jnp.concatenate(own, axis=0), window(own, y, 4)
    pair, own, turned = lax.optimization_barrier((pair, own, turned))
    early = lax.optimization_barrier(jnp.concatenate([pair, far], axis=0))
    pieces = matmul(own, early, ((1,), (1,))).astype(BF)
    late = late_blocks(pair, far)
    first = add(lax.all_to_all(pieces.reshape(4, 128, 768), "y", 0, 0))
    panel = lax.optimization_barrier(jnp.concatenate(late, axis=0))
    pieces = [matmul(rows, panel, ((1,), (1,))).astype(BF) for rows in chunks(turned)]
    pieces[0] = lax.optimization_barrier(pieces[0])
    second = add(scatter(pieces, "y"))
    part = jnp.concatenate([first, second], axis=1)
    panel = jnp.concatenate([early, panel], axis=0)
    part = add(lax.all_to_all(part.reshape(4, 32, 2048), "zh", 0, 0))
    near = lax.all_gather(part, "zh", axis=0, tiled=True)
    after, before = fetch(near, "y", 1), fetch(near, "y", 3)
    sent = lax.optimization_barrier((after[:64], before[64:]))
    far = lax.optimization_barrier((fetch(sent[0], "y", 1), fetch(sent[1], "y", 3)))

    def product(rows):
        return matmul(rows, panel, ((1,), (0,)))

    first = core_sum([(m[:64], m[64:]) for m in map(product, (near, after, before))])
    second = core_sum([(product(far[0]), product(far[1]))])
    inner = window([first[:64], first[64:128], second, first[128:]], back, 4)

    pair, last = pair_of(inner.astype(BF))
    pair, *late = lax.optimization_barrier([pair, last, *late_blocks(pair, last)])
    panels = jnp.concatenate([pair, late[0]], axis=0), jnp.concatenate(late[1:], axis=0)
    gram = [(near[:64], near[64:]), (after[:64], after[64:]), far, (before[:64], before[64:])]
    mixed = []
    for rows in zip(*gram):
        rows = window(rows, back, 4)
        halves = rows[:, :768], rows[:, 768:]
        mixed.append(sum(matmul(h, panel, ((1,), (0,))) for h, panel in zip(halves, panels)))
    mixed = mixed[0] + swap(mixed[1], "core")
    mine = iterate.astype(F32)
    return math.sqrt(COLS) * (coef_a * mine + (coef_b * inner + coef_c * mixed))


def solution(mesh):
    fine = Mesh(mesh.devices.reshape(4, 2, 2, 4, 4), (*ROW, *COL))
    placed = P(ROW, COL)
    return jax.shard_map(
        per_device, mesh=fine, in_specs=(placed,), out_specs=placed, check_vma=False
    )
```

```python
import math

import jax
import jax.numpy as jnp
from jax import lax
from jax.sharding import Mesh
from jax.sharding import PartitionSpec as P

COLS = 8192

coef_a = 3.4445
coef_b = -4.775
coef_c = 2.0315

ROW = ("x", "zl", "core")
COL = ("zh", "y")
BF, F32 = jnp.bfloat16, jnp.float32


def swap(array, axis):
    return lax.ppermute(array, axis, [(0, 1), (1, 0)])


def send(array, axis, k):
    return lax.ppermute(array, axis, [(i, (i + k) % 4) for i in range(4)]) if k else array


def fetch(array, axis, k):
    return send(array, axis, (4 - k) % 4)


def add(got):
    got = [g.astype(F32) for g in got]
    return ((got[0] + got[1]) + (got[2] + got[3])).astype(BF)


def scatter(pieces, axis):
    return [send(pieces[k], axis, k) for k in (0, 1, 3, 2)]


def chunks(array):
    return jnp.split(array, 4, axis=0)


def window(parts, first, count):
    rows = parts[0].shape[0]
    ring = jnp.concatenate([*parts, *parts[: count - 1]], axis=0)
    return lax.dynamic_slice_in_dim(ring, first * rows, count * rows, 0)


def matmul(a, b, dims):
    return lax.dot_general(a, b, (dims, ((), ())), preferred_element_type=F32)


def pair_of(block):
    far = fetch(block, "x", 2)
    return jnp.concatenate([block, swap(block, "zl")], axis=0), far


def late_blocks(pair, far):
    return [fetch(pair, "x", 1), fetch(pair, "x", 3), swap(far, "zl")]


def core_sum(products):
    mine = jnp.concatenate([m for m, _ in products], axis=0)
    other = jnp.concatenate([o for _, o in products], axis=0)
    return mine + swap(other, "core")


def per_device(iterate):
    y, zh = lax.axis_index("y"), lax.axis_index("zh")
    back = lax.rem(4 - y, 4)
    other = swap(iterate, "core")
    pair, far = pair_of(iterate)

    own = [jnp.concatenate(rows, axis=0) for rows in zip(chunks(iterate), chunks(other))]
    own = [window(chunks(rows), zh, 4) for rows in own]
    own, turned = jnp.concatenate(own, axis=0), window(own, y, 4)
    pair, own, turned = lax.optimization_barrier((pair, own, turned))
    early = lax.optimization_barrier(jnp.concatenate([pair, far], axis=0))
    pieces = matmul(own, early, ((1,), (1,))).astype(BF)
    late = late_blocks(pair, far)
    first = add(lax.all_to_all(pieces.reshape(4, 128, 768), "y", 0, 0))
    panel = lax.optimization_barrier(jnp.concatenate(late, axis=0))
    pieces = [matmul(rows, panel, ((1,), (1,))).astype(BF) for rows in chunks(turned)]
    pieces[0] = lax.optimization_barrier(pieces[0])
    second = add(scatter(pieces, "y"))
    part = jnp.concatenate([first, second], axis=1)
    panel = jnp.concatenate([early, panel], axis=0)
    part = add(scatter(chunks(part), "zh"))
    near = lax.all_gather(part, "zh", axis=0, tiled=True)
    after, before = fetch(near, "y", 1), fetch(near, "y", 3)
    sent = lax.optimization_barrier((after[:64], before[64:]))
    far = lax.optimization_barrier((fetch(sent[0], "y", 1), fetch(sent[1], "y", 3)))

    def product(rows):
        return matmul(rows, panel, ((1,), (0,)))

    first = core_sum([(m[:64], m[64:]) for m in map(product, (near, after, before))])
    second = core_sum([(product(far[0]), product(far[1]))])
    inner = window([first[:64], first[64:128], second, first[128:]], back, 4)

    pair, last = lax.optimization_barrier(pair_of(inner.astype(BF)))
    *late, zl_far = late_blocks(pair, last)
    gram = [(near[:64], near[64:]), (after[:64], after[64:]), far, (before[:64], before[64:])]
    gram = [window(rows, back, 4) for rows in zip(*gram)]
    early = jnp.concatenate([pair, last, zl_far], axis=0)
    mixed = [
        matmul(jnp.concatenate([rows[:, :768], rows[:, 1792:]], axis=1), early, ((1,), (0,)))
        for rows in gram
    ]
    *late, mixed_0, mixed_1 = lax.optimization_barrier((*late, *mixed))
    late = jnp.concatenate(late, axis=0)
    mixed = [
        product + matmul(rows[:, 768:1792], late, ((1,), (0,)))
        for product, rows in zip((mixed_0, mixed_1), gram)
    ]
    mixed = mixed[0] + swap(mixed[1], "core")
    mine = iterate.astype(F32)
    return math.sqrt(COLS) * (coef_a * mine + (coef_b * inner + coef_c * mixed))


def solution(mesh):
    fine = Mesh(mesh.devices.reshape(4, 2, 2, 4, 4), (*ROW, *COL))
    placed = P(ROW, COL)
    return jax.shard_map(
        per_device, mesh=fine, in_specs=(placed,), out_specs=placed, check_vma=False
    )
```

```python
import math

import jax
import jax.numpy as jnp
from jax import lax
from jax.sharding import Mesh
from jax.sharding import PartitionSpec as P

COLS = 8192

coef_a = 3.4445
coef_b = -4.775
coef_c = 2.0315

ROW = ("x", "zl", "core")
COL = ("zh", "y")
BF, F32 = jnp.bfloat16, jnp.float32


def swap(array, axis):
    return lax.ppermute(array, axis, [(0, 1), (1, 0)])


def send(array, axis, k):
    return lax.ppermute(array, axis, [(i, (i + k) % 4) for i in range(4)]) if k else array


def fetch(array, axis, k):
    return send(array, axis, (4 - k) % 4)


def add(got):
    got = [g.astype(F32) for g in got]
    return ((got[0] + got[1]) + (got[2] + got[3])).astype(BF)


def scatter(pieces, axis):
    return [send(pieces[k], axis, k) for k in (0, 1, 3, 2)]


def scatter_pairs(pieces, axis):
    return [pieces[0]] + [lax.ppermute(pieces[k], axis, [(i, i ^ k) for i in range(4)]) for k in (1, 3, 2)]


def chunks(array):
    return jnp.split(array, 4, axis=0)


def window(parts, first, count):
    rows = parts[0].shape[0]
    ring = jnp.concatenate([*parts, *parts[: count - 1]], axis=0)
    return lax.dynamic_slice_in_dim(ring, first * rows, count * rows, 0)


def matmul(a, b, dims):
    return lax.dot_general(a, b, (dims, ((), ())), preferred_element_type=F32)


def pair_of(block):
    far = fetch(block, "x", 2)
    return jnp.concatenate([block, swap(block, "zl")], axis=0), far


def late_blocks(pair, far):
    return [fetch(pair, "x", 1), fetch(pair, "x", 3), swap(far, "zl")]


def core_sum(products):
    mine = jnp.concatenate([m for m, _ in products], axis=0)
    other = jnp.concatenate([o for _, o in products], axis=0)
    return mine + swap(other, "core")


def per_device(iterate):
    y, zh = lax.axis_index("y"), lax.axis_index("zh")
    back = lax.rem(4 - y, 4)
    other = swap(iterate, "core")
    pair, far = pair_of(iterate)

    own = [jnp.concatenate(rows, axis=0) for rows in zip(chunks(iterate), chunks(other))]
    own = jnp.stack(own).reshape(4, 4, 32, 512)
    own = [lax.dynamic_slice_in_dim(own, zh ^ k, 1, 1) for k in range(4)]
    own = jnp.concatenate(own, axis=1).reshape(512, 512)
    turned = window(chunks(own), y, 4)
    pair, own, turned = lax.optimization_barrier((pair, own, turned))
    early = lax.optimization_barrier(jnp.concatenate([pair, far], axis=0))
    pieces = matmul(own, early, ((1,), (1,))).astype(BF)
    late = late_blocks(pair, far)
    first = add(lax.all_to_all(pieces.reshape(4, 128, 768), "y", 0, 0))
    panel = lax.optimization_barrier(jnp.concatenate(late, axis=0))
    pieces = [matmul(rows, panel, ((1,), (1,))).astype(BF) for rows in chunks(turned)]
    pieces[0] = lax.optimization_barrier(pieces[0])
    second = add(scatter(pieces, "y"))
    part = jnp.concatenate([first, second], axis=1)
    panel = jnp.concatenate([early, panel], axis=0)
    part = add(scatter_pairs(chunks(part), "zh"))
    near = lax.all_gather(part, "zh", axis=0, tiled=True)
    after, before = fetch(near, "y", 1), fetch(near, "y", 3)
    sent = lax.optimization_barrier((after[:64], before[64:]))
    far = lax.optimization_barrier((fetch(sent[0], "y", 1), fetch(sent[1], "y", 3)))

    def product(rows):
        return matmul(rows, panel, ((1,), (0,)))

    first = core_sum([(m[:64], m[64:]) for m in map(product, (near, after, before))])
    second = core_sum([(product(far[0]), product(far[1]))])
    inner = window([first[:64], first[64:128], second, first[128:]], back, 4)

    pair, last = pair_of(inner.astype(BF))
    pair, *late = lax.optimization_barrier([pair, last, *late_blocks(pair, last)])
    panels = jnp.concatenate([pair, late[0]], axis=0), jnp.concatenate(late[1:], axis=0)
    gram = [(near[:64], near[64:]), (after[:64], after[64:]), far, (before[:64], before[64:])]
    mixed = []
    for rows in zip(*gram):
        rows = window(rows, back, 4)
        halves = rows[:, :768], rows[:, 768:]
        mixed.append(sum(matmul(h, panel, ((1,), (0,))) for h, panel in zip(halves, panels)))
    mixed = mixed[0] + swap(mixed[1], "core")
    mine = iterate.astype(F32)
    return math.sqrt(COLS) * (coef_a * mine + (coef_b * inner + coef_c * mixed))


def solution(mesh):
    fine = Mesh(mesh.devices.reshape(4, 2, 2, 4, 4), (*ROW, *COL))
    placed = P(ROW, COL)
    return jax.shard_map(
        per_device, mesh=fine, in_specs=(placed,), out_specs=placed, check_vma=False
    )
```

```python
import math

import jax
import jax.numpy as jnp
from jax import lax
from jax.sharding import Mesh
from jax.sharding import PartitionSpec as P

COLS = 8192

coef_a = 3.4445
coef_b = -4.775
coef_c = 2.0315

ROW = ("x", "zl", "core")
COL = ("zh", "y")
BF, F32 = jnp.bfloat16, jnp.float32


def swap(array, axis):
    return lax.ppermute(array, axis, [(0, 1), (1, 0)])


def send(array, axis, k):
    return lax.ppermute(array, axis, [(i, (i + k) % 4) for i in range(4)]) if k else array


def fetch(array, axis, k):
    return send(array, axis, (4 - k) % 4)


def add(got):
    got = [g.astype(F32) for g in got]
    return ((got[0] + got[1]) + (got[2] + got[3])).astype(BF)


def scatter_pairs(pieces, axis):
    return [pieces[0]] + [lax.ppermute(pieces[k], axis, [(i, i ^ k) for i in range(4)]) for k in (1, 3, 2)]


def chunks(array):
    return jnp.split(array, 4, axis=0)


def window(parts, first, count):
    rows = parts[0].shape[0]
    ring = jnp.concatenate([*parts, *parts[: count - 1]], axis=0)
    return lax.dynamic_slice_in_dim(ring, first * rows, count * rows, 0)


def matmul(a, b, dims):
    return lax.dot_general(a, b, (dims, ((), ())), preferred_element_type=F32)


def pair_of(block):
    far = fetch(block, "x", 2)
    return jnp.concatenate([block, swap(block, "zl")], axis=0), far


def late_blocks(pair, far):
    return [fetch(pair, "x", 1), fetch(pair, "x", 3), swap(far, "zl")]


def core_sum(products):
    mine = jnp.concatenate([m for m, _ in products], axis=0)
    other = jnp.concatenate([o for _, o in products], axis=0)
    return mine + swap(other, "core")


def per_device(iterate):
    y, zh = lax.axis_index("y"), lax.axis_index("zh")
    back = lax.rem(4 - y, 4)
    other = swap(iterate, "core")
    pair, far = pair_of(iterate)

    own = [jnp.concatenate(rows, axis=0) for rows in zip(chunks(iterate), chunks(other))]
    own = jnp.stack(own).reshape(4, 4, 32, 512)
    own = [lax.dynamic_slice_in_dim(own, zh ^ k, 1, 1) for k in range(4)]
    own = jnp.concatenate(own, axis=1).reshape(512, 512)
    turned = [lax.dynamic_slice_in_dim(own, (y ^ k) * 128, 128) for k in range(4)]
    turned = jnp.concatenate(turned, axis=0)
    pair, own, turned = lax.optimization_barrier((pair, own, turned))
    early = lax.optimization_barrier(jnp.concatenate([pair, far], axis=0))
    pieces = matmul(own, early, ((1,), (1,))).astype(BF)
    late = late_blocks(pair, far)
    first = add(lax.all_to_all(pieces.reshape(4, 128, 768), "y", 0, 0))
    panel = lax.optimization_barrier(jnp.concatenate(late, axis=0))
    pieces = [matmul(rows, panel, ((1,), (1,))).astype(BF) for rows in chunks(turned)]
    pieces[0] = lax.optimization_barrier(pieces[0])
    second = add(scatter_pairs(pieces, "y"))
    part = jnp.concatenate([first, second], axis=1)
    panel = jnp.concatenate([early, panel], axis=0)
    part = add(scatter_pairs(chunks(part), "zh"))
    near = lax.all_gather(part, "zh", axis=0, tiled=True)
    after, before = fetch(near, "y", 1), fetch(near, "y", 3)
    sent = lax.optimization_barrier((after[:64], before[64:]))
    far = lax.optimization_barrier((fetch(sent[0], "y", 1), fetch(sent[1], "y", 3)))

    def product(rows):
        return matmul(rows, panel, ((1,), (0,)))

    first = core_sum([(m[:64], m[64:]) for m in map(product, (near, after, before))])
    second = core_sum([(product(far[0]), product(far[1]))])
    inner = window([first[:64], first[64:128], second, first[128:]], back, 4)

    pair, last = pair_of(inner.astype(BF))
    pair, *late = lax.optimization_barrier([pair, last, *late_blocks(pair, last)])
    panels = jnp.concatenate([pair, late[0]], axis=0), jnp.concatenate(late[1:], axis=0)
    gram = [(near[:64], near[64:]), (after[:64], after[64:]), far, (before[:64], before[64:])]
    mixed = []
    for rows in zip(*gram):
        rows = window(rows, back, 4)
        halves = rows[:, :768], rows[:, 768:]
        mixed.append(sum(matmul(h, panel, ((1,), (0,))) for h, panel in zip(halves, panels)))
    mixed = mixed[0] + swap(mixed[1], "core")
    mine = iterate.astype(F32)
    return math.sqrt(COLS) * (coef_a * mine + (coef_b * inner + coef_c * mixed))


def solution(mesh):
    fine = Mesh(mesh.devices.reshape(4, 2, 2, 4, 4), (*ROW, *COL))
    placed = P(ROW, COL)
    return jax.shard_map(
        per_device, mesh=fine, in_specs=(placed,), out_specs=placed, check_vma=False
    )
```

```python
import math

import jax
import jax.numpy as jnp
from jax import lax
from jax.sharding import Mesh
from jax.sharding import PartitionSpec as P

COLS = 8192

coef_a = 3.4445
coef_b = -4.775
coef_c = 2.0315

ROW = ("x", "zl", "core")
COL = ("zh", "y")
BF, F32 = jnp.bfloat16, jnp.float32


def swap(array, axis):
    return lax.ppermute(array, axis, [(0, 1), (1, 0)])


def send(array, axis, k):
    return lax.ppermute(array, axis, [(i, (i + k) % 4) for i in range(4)]) if k else array


def fetch(array, axis, k):
    return send(array, axis, (4 - k) % 4)


def add(got):
    got = [g.astype(F32) for g in got]
    return ((got[0] + got[1]) + (got[2] + got[3])).astype(BF)


def trade(array, axis, k):
    return lax.ppermute(array, axis, [(i, i ^ k) for i in range(4)])


def scatter_pairs(pieces, axis):
    return [pieces[0]] + [trade(pieces[k], axis, k) for k in (1, 3, 2)]


def chunks(array):
    return jnp.split(array, 4, axis=0)


def window(parts, first, count):
    rows = parts[0].shape[0]
    ring = jnp.concatenate([*parts, *parts[: count - 1]], axis=0)
    return lax.dynamic_slice_in_dim(ring, first * rows, count * rows, 0)


def matmul(a, b, dims):
    return lax.dot_general(a, b, (dims, ((), ())), preferred_element_type=F32)


def pair_of(block):
    far = fetch(block, "x", 2)
    return jnp.concatenate([block, swap(block, "zl")], axis=0), far


def late_blocks(pair, far):
    return [trade(pair, "x", 1), trade(pair, "x", 3), swap(far, "zl")]


def core_sum(products):
    mine = jnp.concatenate([m for m, _ in products], axis=0)
    other = jnp.concatenate([o for _, o in products], axis=0)
    return mine + swap(other, "core")


def per_device(iterate):
    y, zh = lax.axis_index("y"), lax.axis_index("zh")
    back = lax.rem(4 - y, 4)
    other = swap(iterate, "core")
    pair, far = pair_of(iterate)

    own = [jnp.concatenate(rows, axis=0) for rows in zip(chunks(iterate), chunks(other))]
    own = jnp.stack(own).reshape(4, 4, 32, 512)
    own = [lax.dynamic_slice_in_dim(own, zh ^ k, 1, 1) for k in range(4)]
    own = jnp.concatenate(own, axis=1).reshape(512, 512)
    turned = [lax.dynamic_slice_in_dim(own, (y ^ k) * 128, 128) for k in range(4)]
    turned = jnp.concatenate(turned, axis=0)
    pair, own, turned = lax.optimization_barrier((pair, own, turned))
    early = lax.optimization_barrier(jnp.concatenate([pair, far], axis=0))
    pieces = matmul(own, early, ((1,), (1,))).astype(BF)
    late = late_blocks(pair, far)
    first = add(lax.all_to_all(pieces.reshape(4, 128, 768), "y", 0, 0))
    panel = lax.optimization_barrier(jnp.concatenate(late, axis=0))
    pieces = [matmul(rows, panel, ((1,), (1,))).astype(BF) for rows in chunks(turned)]
    pieces[0] = lax.optimization_barrier(pieces[0])
    second = add(scatter_pairs(pieces, "y"))
    part = jnp.concatenate([first, second], axis=1)
    panel = jnp.concatenate([early, panel], axis=0)
    part = add(scatter_pairs(chunks(part), "zh"))
    near = lax.all_gather(part, "zh", axis=0, tiled=True)
    after, before = fetch(near, "y", 1), fetch(near, "y", 3)
    sent = lax.optimization_barrier((after[:64], before[64:]))
    far = lax.optimization_barrier((fetch(sent[0], "y", 1), fetch(sent[1], "y", 3)))

    def product(rows):
        return matmul(rows, panel, ((1,), (0,)))

    first = core_sum([(m[:64], m[64:]) for m in map(product, (near, after, before))])
    second = core_sum([(product(far[0]), product(far[1]))])
    inner = window([first[:64], first[64:128], second, first[128:]], back, 4)

    pair, last = pair_of(inner.astype(BF))
    pair, *late = lax.optimization_barrier([pair, last, *late_blocks(pair, last)])
    panels = jnp.concatenate([pair, late[0]], axis=0), jnp.concatenate(late[1:], axis=0)
    gram = [(near[:64], near[64:]), (after[:64], after[64:]), far, (before[:64], before[64:])]
    mixed = []
    for rows in zip(*gram):
        rows = window(rows, back, 4)
        halves = rows[:, :768], rows[:, 768:]
        mixed.append(sum(matmul(h, panel, ((1,), (0,))) for h, panel in zip(halves, panels)))
    mixed = mixed[0] + swap(mixed[1], "core")
    mine = iterate.astype(F32)
    return math.sqrt(COLS) * (coef_a * mine + (coef_b * inner + coef_c * mixed))


def solution(mesh):
    fine = Mesh(mesh.devices.reshape(4, 2, 2, 4, 4), (*ROW, *COL))
    placed = P(ROW, COL)
    return jax.shard_map(
        per_device, mesh=fine, in_specs=(placed,), out_specs=placed, check_vma=False
    )
```
